32 devices in a mesh: tp: 4 (over y, core), ad: 8 (over z, x).
Axes of the slice: x: 2, y: 2, z: 4, core: 2. Of those that a mesh axis runs over, the one named last changes fastest.
Arguments:
- hidden: bfloat16 [2048, 8192], P('ad'), may hold values from -6 to 6
- key_value_weight: bfloat16 [8192, 2048], P(None, 'tp'), may hold values from -0.0625 to 0.0625
- request_group: int32 [2048, 1], P('ad'), may hold values from 0 to 7; in each aligned block of 256 rows (0 to 255, 256 to 511, ...) at most 64 rows name the same one
- request_member: int32 [2048], P('ad'), may hold values from 0 to 3
- adapter_down_weight: bfloat16 [8192, 2048], P('tp', 'ad'), may hold values from -0.0625 to 0.0625
- adapter_up_weight: bfloat16 [2048, 2048], P('ad', 'tp'), may hold values from -0.75 to 0.75
Outputs:
- kv_out: bfloat16 [2048, 2048], P('ad', 'tp')
The draws below stay inside these ranges and needn't reach their ends.
Inputs may be any that keep to these rules, and one draw needn't show every extreme that they name: `request_group`: among the 256 rows of one index of ad, no group is named by more than 64 rows, a bound that some block reaches.
All inputs are finite; a program needn't handle non-finite values.
Results may differ from the reference program's by a relative error of at most 0.007.
Values may be sent and summed in bfloat16 or wider, within the bound.
No kernel may reach another device: no remote copies, remote signals or barrier semaphores. Data moves between devices by JAX's collectives and lax.ppermute only.
A program may use at most 128 MiB of HBM per device.

```python
import math
import jax
import jax.numpy as jnp
import numpy as np
from jax import lax

MODEL_WIDTH = 8192
KEY_VALUE_WIDTH = 1024
ADAPTER_RANK = 64
ADP_DEV = 4
ROWS_DEV = 256
ADAPTER_COUNT = 32
REQUEST_COUNT = 2048
CAP = 64
N_AD = 8


def plant(result, rng, low, high):
    index_at = [jax.random.randint(jax.random.fold_in(rng, axis), (), 0, length) for axis, length in enumerate(result.shape)]
    widest = result.shape.index(max(result.shape))
    next_to = index_at[:widest] + [(index_at[widest] + 1) % result.shape[widest]] + index_at[widest + 1:]
    return result.at[tuple(index_at)].set(low).at[tuple(next_to)].set(high)


def steps_of(rng, shape, cuts, low, high):
    level = 1.0
    for axis_at, blocks in cuts:
        draws = jax.random.uniform(jax.random.fold_in(jax.random.fold_in(rng, 6), axis_at), (blocks,), jnp.float32, low / len(cuts), high / len(cuts))
        level = level * jnp.repeat(jnp.exp(draws), shape[axis_at] // blocks).reshape((-1,) + (1,) * (len(shape) - 1 - axis_at))
    return level


def deal_out(own_key, own, number, rows, number_of, top, most, skew):
    ranking = jax.random.permutation(own_key, number_of)
    packed, ordinary = shares(number_of, rows * top, most, skew, True), shares(number_of, rows * top, most, skew, False)
    places = jnp.arange(number_of)

    def named(sizes, turn):
        used = int((sizes > 0).sum())
        fixed = max(1, used // 4)
        moved = fixed + (places - fixed + turn * (used - fixed)) % max(1, number_of - fixed)
        return jnp.zeros((number_of,), jnp.int32).at[ranking[jnp.where(places < fixed, places, moved)]].set(jnp.asarray(sizes, jnp.int32))

    sizes = jnp.where(number % 4 == 0, named(packed, number // 4), named(ordinary, number - number // 4 - 1))
    mixed = jax.random.permutation(jax.random.fold_in(own, 3), number_of)
    giver, taker = mixed[0:number_of // 2 * 2:2], mixed[1:number_of // 2 * 2:2]
    slack = jnp.minimum(sizes[giver] - 1, most - sizes[taker]) // 2
    slack = jnp.where((giver == ranking[0]) | (taker == ranking[0]) | (sizes[taker] == 0), 0, jnp.maximum(slack, 0))
    moved = jax.random.randint(jax.random.fold_in(own, 4), (number_of // 2,), 0, 1 << 20) % (slack + 1)
    sizes = sizes.at[giver].add(-moved).at[taker].add(moved)
    members = jnp.searchsorted(jnp.cumsum(sizes), jnp.arange(rows * top), side="right").astype(jnp.int32)
    listing = members.reshape(top, rows).T
    listing = listing[jax.random.permutation(jax.random.fold_in(own, 1), rows)]
    turn = jax.random.randint(jax.random.fold_in(own, 2), (rows, 1), 0, top)
    return jnp.take_along_axis(listing, (jnp.arange(top)[None, :] + turn) % top, axis=1)


def shares(amount, total, bound, slope, full):
    portions = [(1 << 20) // math.isqrt(rank ** slope) + 1 for rank in range(1, amount + 1)]
    largest = bound if full else min(bound, max(-(-total // amount), total * portions[0] // sum(portions)))
    least = 1 if total - largest >= amount - 1 else 0
    holding, rest = [largest] + [least] * (amount - 1), total - largest - least * (amount - 1)
    while rest > 0:
        movable = [i for i in range(1, amount) if holding[i] < largest] or [i for i in range(1, amount) if holding[i] < bound]
        mass, remaining = sum([portions[i] for i in movable]), rest
        for i in movable:
            addition = min(bound - holding[i], max(1, remaining * portions[i] // mass), rest)
            holding[i] = holding[i] + addition
            rest = rest - addition
    return np.array(holding)


def gaussian(rng, dims, scale, limit, shards=(), dtype=jnp.bfloat16):
    level = steps_of(rng, dims, shards, -0.22, 0.18) if shards else 1.0
    drawn = jax.random.normal(rng, dims, jnp.float32) * scale * level
    return jnp.minimum(jnp.maximum(drawn, -limit), limit).astype(dtype)


def setup_inputs(seed: int = 0) -> dict:
    arg_keys = jax.random.split(jax.random.key(seed), 7)
    hidden = gaussian(arg_keys[0], (REQUEST_COUNT, MODEL_WIDTH), 1.0, 6.0, ((0, 8),))
    key_value_weight = gaussian(arg_keys[1], (MODEL_WIDTH, 2 * KEY_VALUE_WIDTH), MODEL_WIDTH ** -0.5, 0.0625, ((1, 4),))
    request_group_keys = jax.random.split(jax.random.fold_in(arg_keys[2], 1), REQUEST_COUNT // ROWS_DEV)
    request_group_turns = jax.random.permutation(jax.random.fold_in(arg_keys[2], 3), REQUEST_COUNT // ROWS_DEV)
    request_group = jax.vmap(lambda own, number: deal_out(jax.random.fold_in(arg_keys[2], 2), own, number, ROWS_DEV, N_AD, 1, CAP, 2))(request_group_keys, request_group_turns).reshape((REQUEST_COUNT, 1))
    request_member = plant(jax.random.randint(arg_keys[3], (REQUEST_COUNT,), 0, ADP_DEV), jax.random.fold_in(arg_keys[3], 1), 0, ADP_DEV - 1).astype(jnp.int32)
    adapter_down_weight = gaussian(arg_keys[4], (MODEL_WIDTH, ADAPTER_COUNT * ADAPTER_RANK), MODEL_WIDTH ** -0.5, 0.0625, ((0, 4), (1, 8)))
    adapter_up_weight = gaussian(arg_keys[5], (ADAPTER_COUNT * ADAPTER_RANK, 2 * KEY_VALUE_WIDTH), ADAPTER_RANK ** -0.5, 0.75, ((0, 8), (1, 4)))
    return dict(hidden=hidden, key_value_weight=key_value_weight, request_group=request_group, request_member=request_member, adapter_down_weight=adapter_down_weight, adapter_up_weight=adapter_up_weight)


def reference(hidden, key_value_weight, request_group, request_member, adapter_down_weight, adapter_up_weight):
    base_output = jnp.dot(hidden, key_value_weight, preferred_element_type=jnp.float32)
    adapter_index = (request_group[:, 0] * ADP_DEV + request_member).astype(jnp.int32)
    down_matrix = adapter_down_weight.reshape(MODEL_WIDTH, ADAPTER_COUNT, ADAPTER_RANK)
    up_matrix = adapter_up_weight.reshape(ADAPTER_COUNT, ADAPTER_RANK, 2 * KEY_VALUE_WIDTH)
    block_total = REQUEST_COUNT // 16
    row_groupings = hidden.reshape(block_total, 16, MODEL_WIDTH)
    block_indices = adapter_index.reshape(block_total, 16)

    def block_quota(inputs):
        rows_block, ids_block = inputs
        down_rows = jnp.take(down_matrix, ids_block, axis=1)
        rank_values = jnp.einsum('rd,drk->rk', rows_block.astype(jnp.float32), down_rows.astype(jnp.float32)).astype(jnp.bfloat16)
        up_rows = jnp.take(up_matrix, ids_block, axis=0)
        return jnp.einsum('rk,rkv->rv', rank_values.astype(jnp.float32), up_rows.astype(jnp.float32)).astype(jnp.bfloat16)

    adapter_update = lax.map(block_quota, (row_groupings, block_indices)).reshape(REQUEST_COUNT, 2 * KEY_VALUE_WIDTH)
    return (base_output + adapter_update.astype(jnp.float32)).astype(jnp.bfloat16)
```

```python
import functools

import jax
import jax.numpy as jnp
from jax import lax
from jax.experimental import pallas as pl
from jax.experimental.pallas import tpu as pltpu
from jax.sharding import PartitionSpec as P

ADAPTER_RANK = 64
LANES = 128


def whole(shape):
    return pl.BlockSpec(shape, lambda *_: (0,) * len(shape))


def pack_kernel(n, cap, at_ref, group_ref, member_ref, rows_ref, spread_ref, *block_refs):
    rows, width = rows_ref.shape
    slots = n * cap
    me = at_ref[1]
    group = group_ref[...]
    by_group = (lax.broadcasted_iota(jnp.int32, (LANES, rows), 0) == group).astype(jnp.float32)
    earlier = (
        lax.broadcasted_iota(jnp.int32, (rows, rows), 0)
        < lax.broadcasted_iota(jnp.int32, (rows, rows), 1)
    ).astype(jnp.bfloat16)
    before = jnp.dot(
        by_group.astype(jnp.bfloat16), earlier, preferred_element_type=jnp.float32
    )
    position = jnp.sum(by_group * before, axis=0, keepdims=True).astype(jnp.int32)
    apart = group ^ me
    half = n // 2
    slot = (apart & (half - 1)) * (2 * cap) + jnp.where(apart >= half, cap, 0) + position
    chosen = lax.broadcasted_iota(jnp.int32, (slots, rows), 0) == slot
    select = chosen.astype(jnp.bfloat16)
    code = jnp.sum(
        jnp.where(chosen, member_ref[...].astype(jnp.float32), 0.0), axis=1, keepdims=True
    )
    code = jnp.broadcast_to(code, (slots, LANES)).astype(jnp.bfloat16)
    packed = jnp.dot(select, rows_ref[...], preferred_element_type=jnp.float32)
    packed = packed.astype(jnp.bfloat16)
    for k, block_ref in enumerate(block_refs):
        block_ref[:, :width] = packed[k * 2 * cap : (k + 1) * 2 * cap]
        block_ref[:, width:] = code[k * 2 * cap : (k + 1) * 2 * cap]
    column = jnp.transpose(jnp.broadcast_to(slot.astype(jnp.float32), (LANES, rows)))[:, :1]
    spread_ref[...] = (
        lax.broadcasted_iota(jnp.int32, (rows, slots), 1).astype(jnp.float32) == column
    ).astype(jnp.bfloat16)


def pack(at, group, member, hidden, width, n, cap):
    rows = hidden.shape[0]
    half = n // 2
    return pl.pallas_call(
        functools.partial(pack_kernel, n, cap),
        grid_spec=pltpu.PrefetchScalarGridSpec(
            num_scalar_prefetch=1,
            grid=(1,),
            in_specs=[
                whole((1, rows)),
                whole((1, rows)),
                pl.BlockSpec((rows, width), lambda i, at: (0, at[0])),
            ],
            out_specs=[whole((rows, n * cap))] + [whole((2 * cap, width + LANES))] * half,
        ),
        out_shape=[jax.ShapeDtypeStruct((rows, n * cap), jnp.bfloat16)]
        + [jax.ShapeDtypeStruct((2 * cap, width + LANES), jnp.bfloat16)] * half,
        name="pack",
    )(at, group, member, hidden)


def score_kernel(pool, count, *refs):
    block_refs, (down_ref, partial_ref, code_ref) = refs[:count], refs[count:]
    width = down_ref.shape[0]
    rows = jnp.concatenate([ref[:, :width] for ref in block_refs], axis=0)
    code = jnp.concatenate([ref[:, width:] for ref in block_refs], axis=0)
    code_ref[...] = code
    member = code.astype(jnp.float32)
    scores = jnp.dot(rows, down_ref[...], preferred_element_type=jnp.float32)
    total = scores.shape[0]
    upper = lax.broadcasted_iota(jnp.int32, (total, LANES), 1) >= ADAPTER_RANK
    kept = jnp.zeros((total, LANES), jnp.float32)
    for pair in range(pool // 2):
        wanted = jnp.where(upper, 2.0 * pair + 1.0, 2.0 * pair)
        kept = kept + jnp.where(
            member == wanted, scores[:, pair * LANES : (pair + 1) * LANES], 0.0
        )
    both = kept + pltpu.roll(kept, ADAPTER_RANK, 1)
    partial_ref[...] = jnp.where(
        upper[: total // 2], both[total // 2 :], both[: total // 2]
    )


def score(blocks, down, late, cap, pool):
    count = len(blocks)
    width, columns = down.shape
    total = count * cap
    return pl.pallas_call(
        functools.partial(score_kernel, pool, count),
        grid=(1,),
        in_specs=[pl.BlockSpec((cap, width + LANES), lambda i: (late, 0))] * count
        + [whole((width, columns))],
        out_specs=[whole((total // 2, LANES)), whole((total, LANES))],
        out_shape=[
            jax.ShapeDtypeStruct((total // 2, LANES), jnp.float32),
            jax.ShapeDtypeStruct((total, LANES), jnp.bfloat16),
        ],
        name="score_late" if late else "score",
    )(*blocks, down)


def raise_kernel(pool, count, *refs):
    partial_refs = refs[:count]
    code_ref, up_ref, *out_refs = refs[count:]
    ranks = partial_refs[0][...]
    for ref in partial_refs[1:]:
        ranks = ranks + ref[...]
    lines = ranks.shape[0]
    upper = lax.broadcasted_iota(jnp.int32, (lines, LANES), 1) >= ADAPTER_RANK
    turned = pltpu.roll(ranks, ADAPTER_RANK, 1)
    ranks = jnp.concatenate(
        [jnp.where(upper, turned, ranks), jnp.where(upper, ranks, turned)], axis=0
    )
    member = code_ref[...].astype(jnp.float32)
    upper = lax.broadcasted_iota(jnp.int32, ranks.shape, 1) >= ADAPTER_RANK
    placed = [
        jnp.where(member == jnp.where(upper, 2.0 * pair + 1.0, 2.0 * pair), ranks, 0.0)
        for pair in range(pool // 2)
    ]
    placed = jnp.concatenate(placed, axis=1).astype(jnp.bfloat16)
    raised = jnp.dot(placed, up_ref[...], preferred_element_type=jnp.float32)
    raised = raised.astype(jnp.bfloat16)
    cap = out_refs[0].shape[0]
    for k, ref in enumerate(out_refs):
        ref[...] = raised[k * cap : (k + 1) * cap]


def raise_ranks(partials, code, up, cap, pool, late):
    count = code.shape[0] // cap
    lines, columns = up.shape
    return pl.pallas_call(
        functools.partial(raise_kernel, pool, len(partials)),
        out_shape=[jax.ShapeDtypeStruct((cap, columns), jnp.bfloat16)] * count,
        name="raise_late" if late else "raise",
    )(*partials, code, up)


def join_kernel(spread_ref, base_ref, *refs):
    block_refs, out_ref = refs[:-1], refs[-1]
    blocks = jnp.concatenate([ref[...] for ref in block_refs], axis=0)
    update = jnp.dot(spread_ref[...], blocks, preferred_element_type=jnp.float32)
    out_ref[...] = (base_ref[...] + update).astype(jnp.bfloat16)


def join(spread, base, blocks):
    return pl.pallas_call(
        join_kernel,
        out_shape=jax.ShapeDtypeStruct(base.shape, jnp.bfloat16),
        name="join",
    )(spread, base, *blocks)


def swap(value, axis, size, apart):
    return lax.ppermute(value, axis, [(i, i ^ apart) for i in range(size)])


def shards(
    n_ad, n_tp, hidden, key_value_weight, request_group, request_member, down, up
):
    rows = hidden.shape[0]
    width, pool = down.shape[0], down.shape[1] // ADAPTER_RANK
    cap = 2 * rows // n_ad
    half = n_ad // 2
    far_down = swap(down, "ad", n_ad, half)
    far_up = swap(up, "ad", n_ad, half)
    at = jnp.stack([lax.axis_index("tp"), lax.axis_index("ad")]).astype(jnp.int32)
    spread, *blocks = pack(
        at, request_group.reshape(1, rows), request_member.reshape(1, rows), hidden, width, n_ad, cap
    )
    taken = [blocks[0]] + [swap(blocks[k], "ad", n_ad, k) for k in range(1, half)]
    base = jnp.dot(hidden, key_value_weight, preferred_element_type=jnp.float32)

    def correction(late, down, up):
        partial, code = score(taken, down, late, cap, pool)
        partials = [partial] + [swap(partial, "tp", n_tp, j) for j in range(1, n_tp)]
        raised = raise_ranks(partials, code, up, cap, pool, late)
        return [raised[0]] + [swap(raised[k], "ad", n_ad, k) for k in range(1, half)]

    near = correction(0, down, up)
    far = correction(1, far_down, far_up)
    ordered = [block for pair in zip(near, far) for block in pair]
    return join(spread, base, ordered)


def solution(mesh):
    placed = (P("ad", None), P(None, "tp"), P("ad", None), P("ad"), P("tp", "ad"), P("ad", "tp"))
    return jax.shard_map(
        functools.partial(shards, mesh.shape["ad"], mesh.shape["tp"]),
        mesh=mesh,
        in_specs=placed,
        out_specs=P("ad", "tp"),
        check_vma=False,
    )
```

```python
import functools

import jax
import jax.numpy as jnp
from jax import lax
from jax.experimental import pallas as pl
from jax.experimental.pallas import tpu as pltpu
from jax.sharding import PartitionSpec as P

ADAPTER_RANK = 64
LANES = 128
IN_HBM = pl.BlockSpec(memory_space=pltpu.HBM)
IN_VMEM = pl.BlockSpec(memory_space=pltpu.VMEM)


def resident(value):
    return pltpu.with_memory_space_constraint(value, pltpu.VMEM)


def resident_call(kernel, outs, name):
    def call(*operands):
        return pl.pallas_call(
            kernel,
            in_specs=[IN_VMEM] * len(operands),
            out_specs=[IN_VMEM] * len(outs),
            out_shape=[pltpu.VMEM(*out) for out in outs],
            name=name,
        )(*map(resident, operands))

    return call


def pack_kernel(
    n, far, cap, group_ref, member_ref, hidden_ref, near_ref, far_ref, *refs
):
    block_refs, (rows_ref, sem) = refs[:-2], refs[-2:]
    rows, width = rows_ref.shape
    slots = n * cap
    half = n // 2
    at = pl.multiple_of(lax.axis_index("tp") * width, LANES)
    copy = pltpu.make_async_copy(hidden_ref.at[:, pl.ds(at, width)], rows_ref, sem)
    copy.start()
    group = group_ref[...]
    by_group = (lax.broadcasted_iota(jnp.int32, (LANES, rows), 0) == group).astype(jnp.float32)
    earlier = (
        lax.broadcasted_iota(jnp.int32, (rows, rows), 0)
        < lax.broadcasted_iota(jnp.int32, (rows, rows), 1)
    ).astype(jnp.bfloat16)
    before = jnp.dot(
        by_group.astype(jnp.bfloat16), earlier, preferred_element_type=jnp.float32
    )
    position = jnp.sum(by_group * before, axis=0, keepdims=True).astype(jnp.int32)
    apart = group ^ lax.axis_index("ad")
    slot = jnp.where(apart < half, apart, half + (apart ^ far)) * cap + position
    chosen = lax.broadcasted_iota(jnp.int32, (slots, rows), 0) == slot
    code = jnp.sum(
        jnp.where(chosen, member_ref[...].astype(jnp.float32), 0.0), axis=1, keepdims=True
    )
    code = jnp.broadcast_to(code, (slots, LANES)).astype(jnp.bfloat16)
    select = chosen.astype(jnp.bfloat16)
    copy.wait()
    packed = jnp.dot(select, rows_ref[...], preferred_element_type=jnp.float32)
    packed = packed.astype(jnp.bfloat16)
    for k, block_ref in enumerate(block_refs):
        block_ref[:, :width] = packed[k * cap : (k + 1) * cap]
        block_ref[:, width:] = code[k * cap : (k + 1) * cap]
    column = jnp.transpose(jnp.broadcast_to(slot.astype(jnp.float32), (LANES, rows)))[:, :1]
    at_slot = lax.broadcasted_iota(jnp.int32, (rows, half * cap), 1).astype(jnp.float32)
    near_ref[...] = (at_slot == column).astype(jnp.bfloat16)
    far_ref[...] = (at_slot + float(half * cap) == column).astype(jnp.bfloat16)


def pack(group, member, hidden, width, n, far, cap):
    rows = hidden.shape[0]
    spread = pltpu.VMEM((rows, n // 2 * cap), jnp.bfloat16)
    block = pltpu.VMEM((cap, width + LANES), jnp.bfloat16)
    return pl.pallas_call(
        functools.partial(pack_kernel, n, far, cap),
        in_specs=[IN_VMEM, IN_VMEM, IN_HBM],
        out_specs=[IN_VMEM] * (2 + n),
        out_shape=[spread] * 2 + [block] * n,
        scratch_shapes=[pltpu.VMEM((rows, width), jnp.bfloat16), pltpu.SemaphoreType.DMA],
        name="pack",
    )(group, member, hidden)


def score_kernel(pool, count, *refs):
    block_refs, (down_ref, partial_ref, code_ref) = refs[:count], refs[count:]
    width = down_ref.shape[0]
    rows = jnp.concatenate([ref[:, :width] for ref in block_refs], axis=0)
    code = jnp.concatenate([ref[:, width:] for ref in block_refs], axis=0)
    code_ref[...] = code
    member = code.astype(jnp.float32)
    scores = jnp.dot(rows, down_ref[...], preferred_element_type=jnp.float32)
    total = scores.shape[0]
    upper = lax.broadcasted_iota(jnp.int32, (total, LANES), 1) >= ADAPTER_RANK
    kept = jnp.zeros((total, LANES), jnp.float32)
    for pair in range(pool // 2):
        wanted = jnp.where(upper, 2.0 * pair + 1.0, 2.0 * pair)
        kept = kept + jnp.where(
            member == wanted, scores[:, pair * LANES : (pair + 1) * LANES], 0.0
        )
    both = kept + pltpu.roll(kept, ADAPTER_RANK, 1)
    partial_ref[...] = jnp.where(
        upper[: total // 2], both[total // 2 :], both[: total // 2]
    )


def score(blocks, down, pool, name):
    total = len(blocks) * blocks[0].shape[0]
    return resident_call(
        functools.partial(score_kernel, pool, len(blocks)),
        [((total // 2, LANES), jnp.float32), ((total, LANES), jnp.bfloat16)],
        name,
    )(*blocks, down)


def raise_kernel(pool, count, *refs):
    partial_refs, (code_ref, up_ref), out_refs = refs[:count], refs[count : count + 2], refs[count + 2 :]
    ranks = partial_refs[0][...]
    for ref in partial_refs[1:]:
        ranks = ranks + ref[...]
    lines = ranks.shape[0]
    upper = lax.broadcasted_iota(jnp.int32, (lines, LANES), 1) >= ADAPTER_RANK
    turned = pltpu.roll(ranks, ADAPTER_RANK, 1)
    ranks = jnp.concatenate(
        [jnp.where(upper, turned, ranks), jnp.where(upper, ranks, turned)], axis=0
    )
    member = code_ref[...].astype(jnp.float32)
    upper = lax.broadcasted_iota(jnp.int32, ranks.shape, 1) >= ADAPTER_RANK
    placed = [
        jnp.where(member == jnp.where(upper, 2.0 * pair + 1.0, 2.0 * pair), ranks, 0.0)
        for pair in range(pool // 2)
    ]
    placed = jnp.concatenate(placed, axis=1).astype(jnp.bfloat16)
    raised = jnp.dot(placed, up_ref[...], preferred_element_type=jnp.float32)
    raised = raised.astype(jnp.bfloat16)
    cap = out_refs[0].shape[0]
    for k, ref in enumerate(out_refs):
        ref[...] = raised[k * cap : (k + 1) * cap]


def raise_ranks(partials, code, up, cap, pool, name):
    outs = code.shape[0] // cap
    return resident_call(
        functools.partial(raise_kernel, pool, len(partials)),
        [((cap, up.shape[1]), jnp.bfloat16)] * outs,
        name,
    )(*partials, code, up)


def join_kernel(spread_ref, base_ref, *refs):
    block_refs, out_ref = refs[:-1], refs[-1]
    blocks = jnp.concatenate([ref[...] for ref in block_refs], axis=0)
    update = jnp.dot(spread_ref[...], blocks, preferred_element_type=jnp.float32)
    out_ref[...] = (base_ref[...] + update).astype(out_ref.dtype)


def join(spread, base, blocks, dtype, name):
    if dtype == jnp.float32:
        return resident_call(join_kernel, [(base.shape, dtype)], name)(spread, base, *blocks)[0]
    return pl.pallas_call(
        join_kernel,
        in_specs=[IN_VMEM] * (2 + len(blocks)),
        out_shape=jax.ShapeDtypeStruct(base.shape, dtype),
        name=name,
    )(*map(resident, (spread, base, *blocks)))


def swap(value, axis, size, apart):
    return lax.ppermute(value, axis, [(i, i ^ apart) for i in range(size)])


def shards(
    n_ad, n_tp, hidden, key_value_weight, request_group, request_member, down, up
):
    rows = hidden.shape[0]
    width, pool = down.shape[0], down.shape[1] // ADAPTER_RANK
    cap = 2 * rows // n_ad
    half = n_ad // 2
    far = n_ad - 2 if n_ad > 2 else half
    far_down = swap(down, "ad", n_ad, far)
    near_spread, far_spread, *blocks = pack(
        request_group.reshape(1, rows), request_member.reshape(1, rows), hidden, width, n_ad, far, cap
    )
    near_rows = [blocks[0]] + [swap(blocks[k], "ad", n_ad, k) for k in range(1, half)]
    far_rows = [blocks[half]] + [swap(blocks[half + k], "ad", n_ad, k) for k in range(1, half)]
    far_up = swap(up, "ad", n_ad, far)
    base = jnp.dot(hidden, key_value_weight, preferred_element_type=jnp.float32)
    base, *near_rows = lax.optimization_barrier((base, *near_rows))

    def correction(rows_of, down, up, which, hold=()):
        partial, code = score(rows_of, down, pool, "score_" + which)
        partials = [partial] + [swap(partial, "tp", n_tp, j) for j in range(1, n_tp)]
        raised = raise_ranks(partials, code, up, cap, pool, "raise_" + which)
        if hold:
            raised, hold = lax.optimization_barrier((raised, hold))
        return [raised[0]] + [swap(raised[k], "ad", n_ad, k) for k in range(1, half)], hold

    near, far_rows = correction(near_rows, down, up, "near", far_rows)
    base = join(near_spread, base, near, jnp.float32, "join_near")
    far, _ = correction(far_rows, far_down, far_up, "far")
    return join(far_spread, base, far, jnp.bfloat16, "join_far")


def solution(mesh):
    placed = (P("ad", None), P(None, "tp"), P("ad", None), P("ad"), P("tp", "ad"), P("ad", "tp"))
    return jax.shard_map(
        functools.partial(shards, mesh.shape["ad"], mesh.shape["tp"]),
        mesh=mesh,
        in_specs=placed,
        out_specs=P("ad", "tp"),
        check_vma=False,
    )
```

```python
import functools

import jax
import jax.numpy as jnp
from jax import lax
from jax.experimental import pallas as pl
from jax.experimental.pallas import tpu as pltpu
from jax.sharding import PartitionSpec as P

ADAPTER_RANK = 64
LANES = 128
LIMIT = pltpu.CompilerParams(vmem_limit_bytes=12 << 20)
IN_HBM = pl.BlockSpec(memory_space=pltpu.HBM)
IN_VMEM = pl.BlockSpec(memory_space=pltpu.VMEM)


def resident(value):
    return pltpu.with_memory_space_constraint(value, pltpu.VMEM)


def stored(value):
    return pltpu.with_memory_space_constraint(value, pltpu.HBM)


def resident_call(kernel, outs, name):
    def call(*operands):
        return pl.pallas_call(
            kernel,
            in_specs=[IN_VMEM] * len(operands),
            out_specs=[IN_VMEM] * len(outs),
            out_shape=[pltpu.VMEM(*out) for out in outs],
            compiler_params=LIMIT,
            name=name,
        )(*map(resident, operands))

    return call


def pack_kernel(
    n, far, cap, group_hbm, member_hbm, hidden_ref, near_ref, far_ref, *refs
):
    block_refs, (group_ref, member_ref, rows_ref, sems) = refs[:n], refs[n:]
    rows, width = rows_ref.shape
    slots = n * cap
    half = n // 2
    at = pl.multiple_of(lax.axis_index("tp") * width, LANES)
    group_copy = pltpu.make_async_copy(group_hbm, group_ref, sems.at[0])
    member_copy = pltpu.make_async_copy(member_hbm, member_ref, sems.at[1])
    rows_copy = pltpu.make_async_copy(hidden_ref.at[:, pl.ds(at, width)], rows_ref, sems.at[2])
    group_copy.start()
    member_copy.start()
    rows_copy.start()
    group_copy.wait()
    group = group_ref[...]
    by_group = (lax.broadcasted_iota(jnp.int32, (LANES, rows), 0) == group).astype(jnp.float32)
    earlier = (
        lax.broadcasted_iota(jnp.int32, (rows, rows), 0)
        < lax.broadcasted_iota(jnp.int32, (rows, rows), 1)
    ).astype(jnp.bfloat16)
    before = jnp.dot(
        by_group.astype(jnp.bfloat16), earlier, preferred_element_type=jnp.float32
    )
    position = jnp.sum(by_group * before, axis=0, keepdims=True).astype(jnp.int32)
    apart = group ^ lax.axis_index("ad")
    slot = jnp.where(apart < half, apart, half + (apart ^ far)) * cap + position
    chosen = lax.broadcasted_iota(jnp.int32, (slots, rows), 0) == slot
    member_copy.wait()
    code = jnp.sum(
        jnp.where(chosen, member_ref[...].astype(jnp.float32), 0.0), axis=1, keepdims=True
    )
    code = jnp.broadcast_to(code, (slots, LANES)).astype(jnp.bfloat16)
    select = chosen.astype(jnp.bfloat16)
    rows_copy.wait()
    packed = jnp.dot(select, rows_ref[...], preferred_element_type=jnp.float32)
    packed = packed.astype(jnp.bfloat16)
    for k, block_ref in enumerate(block_refs):
        block_ref[:, :width] = packed[k * cap : (k + 1) * cap]
        block_ref[:, width:] = code[k * cap : (k + 1) * cap]
    column = jnp.transpose(jnp.broadcast_to(slot.astype(jnp.float32), (LANES, rows)))[:, :1]
    at_slot = lax.broadcasted_iota(jnp.int32, (rows, half * cap), 1).astype(jnp.float32)
    near_ref[...] = (at_slot == column).astype(jnp.bfloat16)
    far_ref[...] = (at_slot + float(half * cap) == column).astype(jnp.bfloat16)


def pack(group, member, hidden, width, n, far, cap):
    rows = hidden.shape[0]
    spread = pltpu.VMEM((rows, n // 2 * cap), jnp.bfloat16)
    block = pltpu.VMEM((cap, width + LANES), jnp.bfloat16)
    return pl.pallas_call(
        functools.partial(pack_kernel, n, far, cap),
        in_specs=[IN_HBM] * 3,
        out_specs=[IN_VMEM] * (2 + n),
        out_shape=[spread] * 2 + [block] * n,
        scratch_shapes=[
            pltpu.VMEM((1, rows), jnp.int32),
            pltpu.VMEM((1, rows), jnp.int32),
            pltpu.VMEM((rows, width), jnp.bfloat16),
            pltpu.SemaphoreType.DMA((3,)),
        ],
        compiler_params=LIMIT,
        name="pack",
    )(*map(stored, (group, member, hidden)))


def score_kernel(pool, count, *refs):
    block_refs, (down_ref, partial_ref, code_ref) = refs[:count], refs[count:]
    width = down_ref.shape[0]
    rows = jnp.concatenate([ref[:, :width] for ref in block_refs], axis=0)
    code = jnp.concatenate([ref[:, width:] for ref in block_refs], axis=0)
    code_ref[...] = code
    member = code.astype(jnp.float32)
    scores = jnp.dot(rows, down_ref[...], preferred_element_type=jnp.float32)
    total = scores.shape[0]
    upper = lax.broadcasted_iota(jnp.int32, (total, LANES), 1) >= ADAPTER_RANK
    kept = jnp.zeros((total, LANES), jnp.float32)
    for pair in range(pool // 2):
        wanted = jnp.where(upper, 2.0 * pair + 1.0, 2.0 * pair)
        kept = kept + jnp.where(
            member == wanted, scores[:, pair * LANES : (pair + 1) * LANES], 0.0
        )
    both = kept + pltpu.roll(kept, ADAPTER_RANK, 1)
    partial_ref[...] = jnp.where(
        upper[: total // 2], both[total // 2 :], both[: total // 2]
    )


def score(blocks, down, pool, name):
    total = len(blocks) * blocks[0].shape[0]
    return resident_call(
        functools.partial(score_kernel, pool, len(blocks)),
        [((total // 2, LANES), jnp.float32), ((total, LANES), jnp.bfloat16)],
        name,
    )(*blocks, down)


def raise_kernel(pool, count, *refs):
    partial_refs, (code_ref, up_ref), out_refs = refs[:count], refs[count : count + 2], refs[count + 2 :]
    ranks = partial_refs[0][...]
    for ref in partial_refs[1:]:
        ranks = ranks + ref[...]
    lines = ranks.shape[0]
    upper = lax.broadcasted_iota(jnp.int32, (lines, LANES), 1) >= ADAPTER_RANK
    turned = pltpu.roll(ranks, ADAPTER_RANK, 1)
    ranks = jnp.concatenate(
        [jnp.where(upper, turned, ranks), jnp.where(upper, ranks, turned)], axis=0
    )
    member = code_ref[...].astype(jnp.float32)
    upper = lax.broadcasted_iota(jnp.int32, ranks.shape, 1) >= ADAPTER_RANK
    placed = [
        jnp.where(member == jnp.where(upper, 2.0 * pair + 1.0, 2.0 * pair), ranks, 0.0)
        for pair in range(pool // 2)
    ]
    placed = jnp.concatenate(placed, axis=1).astype(jnp.bfloat16)
    raised = jnp.dot(placed, up_ref[...], preferred_element_type=jnp.float32)
    raised = raised.astype(jnp.bfloat16)
    cap = out_refs[0].shape[0]
    for k, ref in enumerate(out_refs):
        ref[...] = raised[k * cap : (k + 1) * cap]


def raise_ranks(partials, code, up, cap, pool, name):
    outs = code.shape[0] // cap
    return resident_call(
        functools.partial(raise_kernel, pool, len(partials)),
        [((cap, up.shape[1]), jnp.bfloat16)] * outs,
        name,
    )(*partials, code, up)


def join_kernel(spread_ref, base_ref, *refs):
    block_refs, out_ref = refs[:-1], refs[-1]
    blocks = jnp.concatenate([ref[...] for ref in block_refs], axis=0)
    update = jnp.dot(spread_ref[...], blocks, preferred_element_type=jnp.float32)
    out_ref[...] = (base_ref[...] + update).astype(out_ref.dtype)


def join(spread, base, blocks, dtype, name):
    if dtype == jnp.float32:
        return resident_call(join_kernel, [(base.shape, dtype)], name)(spread, base, *blocks)[0]
    return pl.pallas_call(
        join_kernel,
        in_specs=[IN_VMEM] * (2 + len(blocks)),
        out_shape=jax.ShapeDtypeStruct(base.shape, dtype),
        compiler_params=LIMIT,
        name=name,
    )(*map(resident, (spread, base, *blocks)))


def base_kernel(hidden_ref, weight_ref, out_ref):
    @pl.when(pl.program_id(0) == 0)
    def _():
        out_ref[...] = jnp.zeros_like(out_ref)

    out_ref[...] += jnp.dot(hidden_ref[...], weight_ref[...], preferred_element_type=jnp.float32)


def base_product(hidden, weight, steps):
    (rows, depth), columns = hidden.shape, weight.shape[1]
    step = depth // steps
    return pl.pallas_call(
        base_kernel,
        grid=(steps,),
        in_specs=[
            pl.BlockSpec((rows, step), lambda i: (0, i)),
            pl.BlockSpec((step, columns), lambda i: (i, 0)),
        ],
        out_specs=pl.BlockSpec((rows, columns), lambda i: (0, 0)),
        out_shape=jax.ShapeDtypeStruct((rows, columns), jnp.float32),
        compiler_params=LIMIT,
        name="base_product",
    )(stored(hidden), stored(weight))


def swap(value, axis, size, apart):
    return lax.ppermute(value, axis, [(i, i ^ apart) for i in range(size)])


def shards(
    n_ad, n_tp, hidden, key_value_weight, request_group, request_member, down, up
):
    rows = hidden.shape[0]
    width, pool = down.shape[0], down.shape[1] // ADAPTER_RANK
    cap = 2 * rows // n_ad
    half = n_ad // 2
    far = n_ad - 2 if n_ad > 2 else half
    far_down = swap(down, "ad", n_ad, far)
    near_spread, far_spread, *blocks = pack(
        request_group.reshape(1, rows), request_member.reshape(1, rows), hidden, width, n_ad, far, cap
    )
    near_rows = [blocks[0]] + [swap(blocks[k], "ad", n_ad, k) for k in range(1, half)]
    far_rows = [blocks[half]] + [swap(blocks[half + k], "ad", n_ad, k) for k in range(1, half)]
    base = base_product(hidden, key_value_weight, 4)
    base, *near_rows = lax.optimization_barrier((base, *near_rows))

    def spread_sum(partial):
        return [partial] + [swap(partial, "tp", n_tp, j) for j in range(1, n_tp)]

    def give_back(raised):
        return [raised[0]] + [swap(raised[k], "ad", n_ad, k) for k in range(half - 1, 0, -1)][::-1]

    partial, code = score(near_rows, down, pool, "score_near")
    partial, late_up = lax.optimization_barrier((partial, up))
    far_up = swap(late_up, "ad", n_ad, far)
    raised = raise_ranks(spread_sum(partial), code, up, cap, pool, "raise_near")
    raised, far_rows = lax.optimization_barrier((raised, far_rows))
    base = join(near_spread, base, give_back(raised), jnp.float32, "join_near")

    partial, code = score(far_rows, far_down, pool, "score_far")
    raised = raise_ranks(spread_sum(partial), code, far_up, cap, pool, "raise_far")
    return join(far_spread, base, give_back(raised), jnp.bfloat16, "join_far")


def solution(mesh):
    placed = (P("ad", None), P(None, "tp"), P("ad", None), P("ad"), P("tp", "ad"), P("ad", "tp"))
    return jax.shard_map(
        functools.partial(shards, mesh.shape["ad"], mesh.shape["tp"]),
        mesh=mesh,
        in_specs=placed,
        out_specs=P("ad", "tp"),
        check_vma=False,
    )
```

```python
import functools

import jax
import jax.numpy as jnp
from jax import lax
from jax.experimental import pallas as pl
from jax.experimental.pallas import tpu as pltpu
from jax.sharding import PartitionSpec as P


ADAPTER_RANK = 64
LANES = 128
LIMIT = pltpu.CompilerParams(vmem_limit_bytes=12 << 20)
IN_HBM = pl.BlockSpec(memory_space=pltpu.HBM)
IN_VMEM = pl.BlockSpec(memory_space=pltpu.VMEM)


def resident(value):
    return pltpu.with_memory_space_constraint(value, pltpu.VMEM)


def stored(value):
    return pltpu.with_memory_space_constraint(value, pltpu.HBM)


def resident_call(kernel, outs):
    def call(*operands):
        return pl.pallas_call(
            kernel,
            in_specs=[IN_VMEM] * len(operands),
            out_specs=[IN_VMEM] * len(outs),
            out_shape=[pltpu.VMEM(*out) for out in outs],
            compiler_params=LIMIT,
        )(*map(resident, operands))

    return call


def pack_kernel(
    n, far, cap, group_hbm, member_hbm, hidden_ref, near_ref, far_ref, *refs
):
    block_refs, (group_ref, member_ref, rows_ref, sems) = refs[:n], refs[n:]
    rows, width = rows_ref.shape
    slots = n * cap
    half = n // 2
    at = pl.multiple_of(lax.axis_index("tp") * width, LANES)
    group_copy = pltpu.make_async_copy(group_hbm, group_ref, sems.at[0])
    member_copy = pltpu.make_async_copy(member_hbm, member_ref, sems.at[1])
    rows_copy = pltpu.make_async_copy(hidden_ref.at[:, pl.ds(at, width)], rows_ref, sems.at[2])
    group_copy.start()
    member_copy.start()
    rows_copy.start()
    group_copy.wait()
    group = group_ref[...]
    by_group = (lax.broadcasted_iota(jnp.int32, (LANES, rows), 0) == group).astype(jnp.float32)
    earlier = (
        lax.broadcasted_iota(jnp.int32, (rows, rows), 0)
        < lax.broadcasted_iota(jnp.int32, (rows, rows), 1)
    ).astype(jnp.bfloat16)
    before = jnp.dot(
        by_group.astype(jnp.bfloat16), earlier, preferred_element_type=jnp.float32
    )
    position = jnp.sum(by_group * before, axis=0, keepdims=True).astype(jnp.int32)
    apart = group ^ lax.axis_index("ad")
    slot = jnp.where(apart < half, apart, half + (apart ^ far)) * cap + position
    chosen = lax.broadcasted_iota(jnp.int32, (slots, rows), 0) == slot
    member_copy.wait()
    code = jnp.sum(
        jnp.where(chosen, member_ref[...].astype(jnp.float32), 0.0), axis=1, keepdims=True
    )
    code = jnp.broadcast_to(code, (slots, LANES)).astype(jnp.bfloat16)
    select = chosen.astype(jnp.bfloat16)
    rows_copy.wait()
    packed = jnp.dot(select, rows_ref[...], preferred_element_type=jnp.float32)
    packed = packed.astype(jnp.bfloat16)
    for k, block_ref in enumerate(block_refs):
        block_ref[:, :width] = packed[k * cap : (k + 1) * cap]
        block_ref[:, width:] = code[k * cap : (k + 1) * cap]
    column = jnp.transpose(jnp.broadcast_to(slot.astype(jnp.float32), (LANES, rows)))[:, :1]
    at_slot = lax.broadcasted_iota(jnp.int32, (rows, half * cap), 1).astype(jnp.float32)
    near_ref[...] = (at_slot == column).astype(jnp.bfloat16)
    far_ref[...] = (at_slot + float(half * cap) == column).astype(jnp.bfloat16)


def pack(group, member, hidden, width, n, far, cap):
    rows = hidden.shape[0]
    spread = pltpu.VMEM((rows, n // 2 * cap), jnp.bfloat16)
    block = pltpu.VMEM((cap, width + LANES), jnp.bfloat16)
    return pl.pallas_call(
        functools.partial(pack_kernel, n, far, cap),
        in_specs=[IN_HBM] * 3,
        out_specs=[IN_VMEM] * (2 + n),
        out_shape=[spread] * 2 + [block] * n,
        scratch_shapes=[
            pltpu.VMEM((1, rows), jnp.int32),
            pltpu.VMEM((1, rows), jnp.int32),
            pltpu.VMEM((rows, width), jnp.bfloat16),
            pltpu.SemaphoreType.DMA((3,)),
        ],
        compiler_params=LIMIT,
        name="pack",
    )(*map(stored, (group, member, hidden)))


def score_kernel(pool, count, *refs):
    block_refs, (down_ref, partial_ref, code_ref) = refs[:count], refs[count:]
    width = down_ref.shape[0]
    rows = jnp.concatenate([ref[:, :width] for ref in block_refs], axis=0)
    code = jnp.concatenate([ref[:, width:] for ref in block_refs], axis=0)
    code_ref[...] = code
    member = code.astype(jnp.float32)
    scores = jnp.dot(rows, down_ref[...], preferred_element_type=jnp.float32)
    total = scores.shape[0]
    upper = lax.broadcasted_iota(jnp.int32, (total, LANES), 1) >= ADAPTER_RANK
    kept = jnp.zeros((total, LANES), jnp.float32)
    for pair in range(pool // 2):
        wanted = jnp.where(upper, 2.0 * pair + 1.0, 2.0 * pair)
        kept = kept + jnp.where(
            member == wanted, scores[:, pair * LANES : (pair + 1) * LANES], 0.0
        )
    both = kept + pltpu.roll(kept, ADAPTER_RANK, 1)
    partial_ref[...] = jnp.where(
        upper[: total // 2], both[total // 2 :], both[: total // 2]
    )


def score(blocks, down, pool):
    total = len(blocks) * blocks[0].shape[0]
    return resident_call(
        functools.partial(score_kernel, pool, len(blocks)),
        [((total // 2, LANES), jnp.float32), ((total, LANES), jnp.bfloat16)],
    )(*blocks, down)


def raise_kernel(pool, count, *refs):
    partial_refs, (code_ref, up_ref), out_refs = refs[:count], refs[count : count + 2], refs[count + 2 :]
    ranks = partial_refs[0][...]
    for ref in partial_refs[1:]:
        ranks = ranks + ref[...]
    lines = ranks.shape[0]
    upper = lax.broadcasted_iota(jnp.int32, (lines, LANES), 1) >= ADAPTER_RANK
    turned = pltpu.roll(ranks, ADAPTER_RANK, 1)
    ranks = jnp.concatenate(
        [jnp.where(upper, turned, ranks), jnp.where(upper, ranks, turned)], axis=0
    )
    member = code_ref[...].astype(jnp.float32)
    upper = lax.broadcasted_iota(jnp.int32, ranks.shape, 1) >= ADAPTER_RANK
    placed = [
        jnp.where(member == jnp.where(upper, 2.0 * pair + 1.0, 2.0 * pair), ranks, 0.0)
        for pair in range(pool // 2)
    ]
    placed = jnp.concatenate(placed, axis=1).astype(jnp.bfloat16)
    raised = jnp.dot(placed, up_ref[...], preferred_element_type=jnp.float32)
    raised = raised.astype(jnp.bfloat16)
    cap = out_refs[0].shape[0]
    for k, ref in enumerate(out_refs):
        ref[...] = raised[k * cap : (k + 1) * cap]


def raise_ranks(partials, code, up, cap, pool):
    outs = code.shape[0] // cap
    return resident_call(
        functools.partial(raise_kernel, pool, len(partials)),
        [((cap, up.shape[1]), jnp.bfloat16)] * outs,
    )(*partials, code, up)


def join_kernel(spread_ref, base_ref, *refs):
    block_refs, out_ref = refs[:-1], refs[-1]
    blocks = jnp.concatenate([ref[...] for ref in block_refs], axis=0)
    update = jnp.dot(spread_ref[...], blocks, preferred_element_type=jnp.float32)
    out_ref[...] = (base_ref[...] + update).astype(out_ref.dtype)


def join(spread, base, blocks, dtype):
    if dtype == jnp.float32:
        return resident_call(join_kernel, [(base.shape, dtype)])(spread, base, *blocks)[0]
    return pl.pallas_call(
        join_kernel,
        in_specs=[IN_VMEM] * (2 + len(blocks)),
        out_shape=jax.ShapeDtypeStruct(base.shape, dtype),
        compiler_params=LIMIT,
    )(*map(resident, (spread, base, *blocks)))


def base_kernel(hidden_ref, weight_ref, out_ref):
    @pl.when(pl.program_id(0) == 0)
    def _():
        out_ref[...] = jnp.zeros_like(out_ref)

    out_ref[...] += jnp.dot(hidden_ref[...], weight_ref[...], preferred_element_type=jnp.float32)


def base_product(hidden, weight, steps):
    (rows, depth), columns = hidden.shape, weight.shape[1]
    step = depth // steps
    return pl.pallas_call(
        base_kernel,
        grid=(steps,),
        in_specs=[
            pl.BlockSpec((rows, step), lambda i: (0, i)),
            pl.BlockSpec((step, columns), lambda i: (i, 0)),
        ],
        out_specs=pl.BlockSpec((rows, columns), lambda i: (0, 0)),
        out_shape=jax.ShapeDtypeStruct((rows, columns), jnp.float32),
        compiler_params=LIMIT,
        name="base_product",
    )(stored(hidden), stored(weight))


def swap(value, axis, size, apart):
    return lax.ppermute(value, axis, [(i, i ^ apart) for i in range(size)])


def shards(
    n_ad, n_tp, hidden, key_value_weight, request_group, request_member, down, up
):
    rows = hidden.shape[0]
    width, pool = down.shape[0], down.shape[1] // ADAPTER_RANK
    cap = 2 * rows // n_ad
    half = n_ad // 2
    far = n_ad - 2 if n_ad > 2 else half
    far_down = swap(down, "ad", n_ad, far)
    near_spread, far_spread, *blocks = pack(
        request_group.reshape(1, rows), request_member.reshape(1, rows), hidden, width, n_ad, far, cap
    )
    near_rows = [blocks[0]] + [swap(blocks[k], "ad", n_ad, k) for k in range(1, half)]
    far_rows = [blocks[half]] + [swap(blocks[half + k], "ad", n_ad, k) for k in range(1, half)]
    base = base_product(hidden, key_value_weight, 4)
    base, *near_rows = lax.optimization_barrier((base, *near_rows))

    def spread_sum(partial):
        return [partial] + [swap(partial, "tp", n_tp, j) for j in range(1, n_tp)]

    def give_back(raised):
        back = [raised[0]]
        for k in range(1, half):
            back.append(swap(raised[k], "ad", n_ad, k))
        return back

    partial, code = score(near_rows, down, pool)
    partial, late_up = lax.optimization_barrier((partial, up))
    far_up = swap(late_up, "ad", n_ad, far)
    raised = raise_ranks(spread_sum(partial), code, up, cap, pool)
    raised, far_rows = lax.optimization_barrier((raised, far_rows))
    base = join(near_spread, base, give_back(raised), jnp.float32)

    partial, code = score(far_rows, far_down, pool)
    raised = raise_ranks(spread_sum(partial), code, far_up, cap, pool)
    return join(far_spread, base, give_back(raised), jnp.bfloat16)


def solution(mesh):
    def step(*arrays):
        return shards(mesh.shape["ad"], mesh.shape["tp"], *arrays)

    placed = (P("ad", None), P(None, "tp"), P("ad", None), P("ad"), P("tp", "ad"), P("ad", "tp"))
    return jax.shard_map(step, mesh=mesh, in_specs=placed, out_specs=P("ad", "tp"), check_vma=False)
```

```python
import functools

import jax
import jax.numpy as jnp
from jax import lax
from jax.experimental import pallas as pl
from jax.experimental.pallas import tpu as pltpu
from jax.sharding import PartitionSpec as P


ADAPTER_RANK = 64
LANES = 128
LIMIT = pltpu.CompilerParams(vmem_limit_bytes=12 << 20)
IN_HBM = pl.BlockSpec(memory_space=pltpu.HBM)
IN_VMEM = pl.BlockSpec(memory_space=pltpu.VMEM)


def resident(value):
    return pltpu.with_memory_space_constraint(value, pltpu.VMEM)


def stored(value):
    return pltpu.with_memory_space_constraint(value, pltpu.HBM)


def resident_call(kernel, outs):
    def call(*operands):
        return pl.pallas_call(
            kernel,
            in_specs=[IN_VMEM] * len(operands),
            out_specs=[IN_VMEM] * len(outs),
            out_shape=[pltpu.VMEM(*out) for out in outs],
            compiler_params=LIMIT,
        )(*map(resident, operands))

    return call


def pack_kernel(
    n, far, cap, group_hbm, member_hbm, hidden_ref, near_ref, far_ref, *refs
):
    block_refs, code_refs = refs[:n], refs[n : n + n // 2]
    group_ref, member_ref, rows_ref, sems = refs[n + n // 2 :]
    rows, width = rows_ref.shape
    slots = n * cap
    half = n // 2
    at = pl.multiple_of(lax.axis_index("tp") * width, LANES)
    group_copy = pltpu.make_async_copy(group_hbm, group_ref, sems.at[0])
    member_copy = pltpu.make_async_copy(member_hbm, member_ref, sems.at[1])
    rows_copy = pltpu.make_async_copy(hidden_ref.at[:, pl.ds(at, width)], rows_ref, sems.at[2])
    group_copy.start()
    member_copy.start()
    rows_copy.start()
    group_copy.wait()
    group = group_ref[...]
    by_group = (lax.broadcasted_iota(jnp.int32, (LANES, rows), 0) == group).astype(jnp.float32)
    earlier = (
        lax.broadcasted_iota(jnp.int32, (rows, rows), 0)
        < lax.broadcasted_iota(jnp.int32, (rows, rows), 1)
    ).astype(jnp.bfloat16)
    before = jnp.dot(
        by_group.astype(jnp.bfloat16), earlier, preferred_element_type=jnp.float32
    )
    position = jnp.sum(by_group * before, axis=0, keepdims=True).astype(jnp.int32)
    apart = group ^ lax.axis_index("ad")
    slot = jnp.where(apart < half, apart, half + (apart ^ far)) * cap + position
    chosen = lax.broadcasted_iota(jnp.int32, (slots, rows), 0) == slot
    select = chosen.astype(jnp.bfloat16)
    member_copy.wait()
    member = jnp.broadcast_to(member_ref[...].astype(jnp.float32), (8, rows)).astype(jnp.bfloat16)
    code = lax.dot_general(
        member, select, (((1,), (1,)), ((), ())), preferred_element_type=jnp.float32
    )
    rows_copy.wait()
    packed = jnp.dot(select, rows_ref[...], preferred_element_type=jnp.float32)
    packed = packed.astype(jnp.bfloat16)
    for k, block_ref in enumerate(block_refs):
        block_ref[...] = packed[k * cap : (k + 1) * cap]
    for k, code_ref in enumerate(code_refs):
        code_ref[:, :cap] = code[:, k * cap : (k + 1) * cap]
        code_ref[:, cap:] = code[:, (half + k) * cap : (half + k + 1) * cap]
    column = jnp.transpose(jnp.broadcast_to(slot.astype(jnp.float32), (LANES, rows)))[:, :1]
    at_slot = lax.broadcasted_iota(jnp.int32, (rows, half * cap), 1).astype(jnp.float32)
    near_ref[...] = (at_slot == column).astype(jnp.bfloat16)
    far_ref[...] = (at_slot + float(half * cap) == column).astype(jnp.bfloat16)


def pack(group, member, hidden, width, n, far, cap):
    rows = hidden.shape[0]
    spread = pltpu.VMEM((rows, n // 2 * cap), jnp.bfloat16)
    block = pltpu.VMEM((cap, width), jnp.bfloat16)
    code = pltpu.VMEM((8, 2 * cap), jnp.float32)
    return pl.pallas_call(
        functools.partial(pack_kernel, n, far, cap),
        in_specs=[IN_HBM] * 3,
        out_specs=[IN_VMEM] * (2 + n + n // 2),
        out_shape=[spread] * 2 + [block] * n + [code] * (n // 2),
        scratch_shapes=[
            pltpu.VMEM((1, rows), jnp.int32),
            pltpu.VMEM((1, rows), jnp.int32),
            pltpu.VMEM((rows, width), jnp.bfloat16),
            pltpu.SemaphoreType.DMA((3,)),
        ],
        compiler_params=LIMIT,
        name="pack",
    )(*map(stored, (group, member, hidden)))


def code_kernel(*refs):
    code_refs, (near_ref, far_ref) = refs[:-2], refs[-2:]
    for k, ref in enumerate(code_refs):
        both = ref.shape[1]
        columns = jnp.transpose(jnp.broadcast_to(ref[:1, :], (LANES, both)))
        part = pl.ds(k * (both // 2), both // 2)
        near_ref[part, :] = columns[: both // 2]
        far_ref[part, :] = columns[both // 2 :]


def spread_codes(codes):
    total = len(codes) * codes[0].shape[1] // 2
    return resident_call(code_kernel, [((total, LANES), jnp.float32)] * 2)(*codes)


def score_kernel(pool, count, *refs):
    block_refs, (code_ref, down_ref, partial_ref) = refs[:count], refs[count:]
    rows = jnp.concatenate([ref[...] for ref in block_refs], axis=0)
    member = code_ref[...]
    scores = jnp.dot(rows, down_ref[...], preferred_element_type=jnp.float32)
    total = scores.shape[0]
    upper = lax.broadcasted_iota(jnp.int32, (total, LANES), 1) >= ADAPTER_RANK
    kept = jnp.zeros((total, LANES), jnp.float32)
    for pair in range(pool // 2):
        wanted = jnp.where(upper, 2.0 * pair + 1.0, 2.0 * pair)
        kept = kept + jnp.where(
            member == wanted, scores[:, pair * LANES : (pair + 1) * LANES], 0.0
        )
    both = kept + pltpu.roll(kept, ADAPTER_RANK, 1)
    partial_ref[...] = jnp.where(
        upper[: total // 2], both[total // 2 :], both[: total // 2]
    )


def score(blocks, code, down, pool):
    total = len(blocks) * blocks[0].shape[0]
    return resident_call(
        functools.partial(score_kernel, pool, len(blocks)), [((total // 2, LANES), jnp.float32)]
    )(*blocks, code, down)[0]


def raise_kernel(pool, count, *refs):
    partial_refs, (code_ref, up_ref), out_refs = refs[:count], refs[count : count + 2], refs[count + 2 :]
    ranks = partial_refs[0][...]
    for ref in partial_refs[1:]:
        ranks = ranks + ref[...]
    lines = ranks.shape[0]
    upper = lax.broadcasted_iota(jnp.int32, (lines, LANES), 1) >= ADAPTER_RANK
    turned = pltpu.roll(ranks, ADAPTER_RANK, 1)
    ranks = jnp.concatenate(
        [jnp.where(upper, turned, ranks), jnp.where(upper, ranks, turned)], axis=0
    )
    member = code_ref[...]
    upper = lax.broadcasted_iota(jnp.int32, ranks.shape, 1) >= ADAPTER_RANK
    placed = [
        jnp.where(member == jnp.where(upper, 2.0 * pair + 1.0, 2.0 * pair), ranks, 0.0)
        for pair in range(pool // 2)
    ]
    placed = jnp.concatenate(placed, axis=1).astype(jnp.bfloat16)
    raised = jnp.dot(placed, up_ref[...], preferred_element_type=jnp.float32)
    raised = raised.astype(jnp.bfloat16)
    cap = out_refs[0].shape[0]
    for k, ref in enumerate(out_refs):
        ref[...] = raised[k * cap : (k + 1) * cap]


def raise_ranks(partials, code, up, cap, pool):
    outs = code.shape[0] // cap
    return resident_call(
        functools.partial(raise_kernel, pool, len(partials)),
        [((cap, up.shape[1]), jnp.bfloat16)] * outs,
    )(*partials, code, up)


def join_kernel(spread_ref, base_ref, *refs):
    block_refs, out_ref = refs[:-1], refs[-1]
    blocks = jnp.concatenate([ref[...] for ref in block_refs], axis=0)
    update = jnp.dot(spread_ref[...], blocks, preferred_element_type=jnp.float32)
    out_ref[...] = (base_ref[...] + update).astype(out_ref.dtype)


def join(spread, base, blocks, dtype):
    if dtype == jnp.float32:
        return resident_call(join_kernel, [(base.shape, dtype)])(spread, base, *blocks)[0]
    return pl.pallas_call(
        join_kernel,
        in_specs=[IN_VMEM] * (2 + len(blocks)),
        out_shape=jax.ShapeDtypeStruct(base.shape, dtype),
        compiler_params=LIMIT,
    )(*map(resident, (spread, base, *blocks)))


def base_kernel(hidden_ref, weight_ref, out_ref):
    @pl.when(pl.program_id(0) == 0)
    def _():
        out_ref[...] = jnp.zeros_like(out_ref)

    out_ref[...] += jnp.dot(hidden_ref[...], weight_ref[...], preferred_element_type=jnp.float32)


def base_product(hidden, weight, steps):
    (rows, depth), columns = hidden.shape, weight.shape[1]
    step = depth // steps
    return pl.pallas_call(
        base_kernel,
        grid=(steps,),
        in_specs=[
            pl.BlockSpec((rows, step), lambda i: (0, i)),
            pl.BlockSpec((step, columns), lambda i: (i, 0)),
        ],
        out_specs=pl.BlockSpec((rows, columns), lambda i: (0, 0)),
        out_shape=jax.ShapeDtypeStruct((rows, columns), jnp.float32),
        compiler_params=LIMIT,
        name="base_product",
    )(stored(hidden), stored(weight))


def swap(value, axis, size, apart):
    return lax.ppermute(value, axis, [(i, i ^ apart) for i in range(size)])


def shards(
    n_ad, n_tp, hidden, key_value_weight, request_group, request_member, down, up
):
    rows = hidden.shape[0]
    width, pool = down.shape[0], down.shape[1] // ADAPTER_RANK
    cap = 2 * rows // n_ad
    half = n_ad // 2
    far = n_ad - 2 if n_ad > 2 else half
    far_down = swap(down, "ad", n_ad, far)
    near_spread, far_spread, *packed = pack(
        request_group.reshape(1, rows), request_member.reshape(1, rows), hidden, width, n_ad, far, cap
    )
    blocks, codes = packed[:n_ad], packed[n_ad:]
    near_rows = [blocks[0]] + [swap(blocks[k], "ad", n_ad, k) for k in range(1, half)]
    far_rows = [blocks[half]] + [swap(blocks[half + k], "ad", n_ad, k) for k in range(1, half)]
    codes = [codes[0]] + [swap(codes[k], "ad", n_ad, k) for k in range(1, half)]
    near_code, far_code = spread_codes(codes)
    base = base_product(hidden, key_value_weight, 4)
    base, *near_rows = lax.optimization_barrier((base, *near_rows))

    def spread_sum(partial):
        return [partial] + [swap(partial, "tp", n_tp, j) for j in range(1, n_tp)]

    def give_back(raised):
        back = [raised[0]]
        for k in range(1, half):
            back.append(swap(raised[k], "ad", n_ad, k))
        return back

    partial = score(near_rows, near_code, down, pool)
    partial, late_up = lax.optimization_barrier((partial, up))
    far_up = swap(late_up, "ad", n_ad, far)
    raised = raise_ranks(spread_sum(partial), near_code, up, cap, pool)
    base = join(near_spread, base, give_back(raised), jnp.float32)

    partial = score(far_rows, far_code, far_down, pool)
    raised = raise_ranks(spread_sum(partial), far_code, far_up, cap, pool)
    return join(far_spread, base, give_back(raised), jnp.bfloat16)


def solution(mesh):
    def step(*arrays):
        return shards(mesh.shape["ad"], mesh.shape["tp"], *arrays)

    placed = (P("ad", None), P(None, "tp"), P("ad", None), P("ad"), P("tp", "ad"), P("ad", "tp"))
    return jax.shard_map(step, mesh=mesh, in_specs=placed, out_specs=P("ad", "tp"), check_vma=False)
```

```python
import functools

import jax
import jax.numpy as jnp
from jax import lax
from jax.experimental import pallas as pl
from jax.experimental.pallas import tpu as pltpu
from jax.sharding import PartitionSpec as P


ADAPTER_RANK = 64
LANES = 128
LIMIT = pltpu.CompilerParams(vmem_limit_bytes=12 << 20)
IN_HBM = pl.BlockSpec(memory_space=pltpu.HBM)
IN_VMEM = pl.BlockSpec(memory_space=pltpu.VMEM)


def resident(value):
    return pltpu.with_memory_space_constraint(value, pltpu.VMEM)


def stored(value):
    return pltpu.with_memory_space_constraint(value, pltpu.HBM)


def resident_call(kernel, outs):
    def call(*operands):
        return pl.pallas_call(
            kernel,
            in_specs=[IN_VMEM] * len(operands),
            out_specs=[IN_VMEM] * len(outs),
            out_shape=[pltpu.VMEM(*out) for out in outs],
            compiler_params=LIMIT,
        )(*map(resident, operands))

    return call


def pack_kernel(
    n, far, cap, group_hbm, member_hbm, hidden_ref, near_ref, far_ref, *refs
):
    block_refs, code_refs = refs[:n], refs[n : n + n // 2]
    group_ref, member_ref, rows_ref, sems = refs[n + n // 2 :]
    rows, width = rows_ref.shape
    slots = n * cap
    half = n // 2
    at = pl.multiple_of(lax.axis_index("tp") * width, LANES)
    group_copy = pltpu.make_async_copy(group_hbm, group_ref, sems.at[0])
    member_copy = pltpu.make_async_copy(member_hbm, member_ref, sems.at[1])
    rows_copy = pltpu.make_async_copy(hidden_ref.at[:, pl.ds(at, width)], rows_ref, sems.at[2])
    group_copy.start()
    member_copy.start()
    rows_copy.start()
    group_copy.wait()
    group = group_ref[...]
    by_group = (lax.broadcasted_iota(jnp.int32, (LANES, rows), 0) == group).astype(jnp.float32)
    earlier = (
        lax.broadcasted_iota(jnp.int32, (rows, rows), 0)
        < lax.broadcasted_iota(jnp.int32, (rows, rows), 1)
    ).astype(jnp.bfloat16)
    before = jnp.dot(
        by_group.astype(jnp.bfloat16), earlier, preferred_element_type=jnp.float32
    )
    position = jnp.sum(by_group * before, axis=0, keepdims=True).astype(jnp.int32)
    apart = group ^ lax.axis_index("ad")
    slot = jnp.where(apart < half, apart, half + (apart ^ far)) * cap + position
    chosen = lax.broadcasted_iota(jnp.int32, (slots, rows), 0) == slot
    select = chosen.astype(jnp.bfloat16)
    member_copy.wait()
    member = jnp.broadcast_to(member_ref[...].astype(jnp.float32), (8, rows)).astype(jnp.bfloat16)
    code = lax.dot_general(
        member, select, (((1,), (1,)), ((), ())), preferred_element_type=jnp.float32
    )
    rows_copy.wait()
    packed = jnp.dot(select, rows_ref[...], preferred_element_type=jnp.float32)
    packed = packed.astype(jnp.bfloat16)
    for k, block_ref in enumerate(block_refs):
        block_ref[...] = packed[k * cap : (k + 1) * cap]
    for k, code_ref in enumerate(code_refs):
        code_ref[:, :cap] = code[:, k * cap : (k + 1) * cap]
        code_ref[:, cap:] = code[:, (half + k) * cap : (half + k + 1) * cap]
    column = jnp.transpose(jnp.broadcast_to(slot.astype(jnp.float32), (LANES, rows)))[:, :1]
    at_slot = lax.broadcasted_iota(jnp.int32, (rows, half * cap), 1).astype(jnp.float32)
    near_ref[...] = (at_slot == column).astype(jnp.bfloat16)
    far_ref[...] = (at_slot + float(half * cap) == column).astype(jnp.bfloat16)


def pack(group, member, hidden, width, n, far, cap):
    rows = hidden.shape[0]
    spread = pltpu.VMEM((rows, n // 2 * cap), jnp.bfloat16)
    block = pltpu.VMEM((cap, width), jnp.bfloat16)
    code = pltpu.VMEM((8, 2 * cap), jnp.float32)
    return pl.pallas_call(
        functools.partial(pack_kernel, n, far, cap),
        in_specs=[IN_HBM] * 3,
        out_specs=[IN_VMEM] * (2 + n + n // 2),
        out_shape=[spread] * 2 + [block] * n + [code] * (n // 2),
        scratch_shapes=[
            pltpu.VMEM((1, rows), jnp.int32),
            pltpu.VMEM((1, rows), jnp.int32),
            pltpu.VMEM((rows, width), jnp.bfloat16),
            pltpu.SemaphoreType.DMA((3,)),
        ],
        compiler_params=LIMIT,
        name="pack",
    )(*map(stored, (group, member, hidden)))


def code_kernel(*refs):
    code_refs, (near_ref, far_ref) = refs[:-2], refs[-2:]
    for k, ref in enumerate(code_refs):
        both = ref.shape[1]
        columns = jnp.transpose(jnp.broadcast_to(ref[:1, :], (LANES, both)))
        part = pl.ds(k * (both // 2), both // 2)
        near_ref[part, :] = columns[: both // 2]
        far_ref[part, :] = columns[both // 2 :]


def spread_codes(codes):
    total = len(codes) * codes[0].shape[1] // 2
    return resident_call(code_kernel, [((total, LANES), jnp.float32)] * 2)(*codes)


def score_kernel(pool, count, *refs):
    block_refs, (code_ref, down_ref, partial_ref) = refs[:count], refs[count:]
    rows = jnp.concatenate([ref[...] for ref in block_refs], axis=0)
    member = code_ref[...]
    scores = jnp.dot(rows, down_ref[...], preferred_element_type=jnp.float32)
    total = scores.shape[0]
    upper = lax.broadcasted_iota(jnp.int32, (total, LANES), 1) >= ADAPTER_RANK
    kept = jnp.zeros((total, LANES), jnp.float32)
    for pair in range(pool // 2):
        wanted = jnp.where(upper, 2.0 * pair + 1.0, 2.0 * pair)
        kept = kept + jnp.where(
            member == wanted, scores[:, pair * LANES : (pair + 1) * LANES], 0.0
        )
    both = kept + pltpu.roll(kept, ADAPTER_RANK, 1)
    partial_ref[...] = jnp.where(
        upper[: total // 2], both[total // 2 :], both[: total // 2]
    )


def score(blocks, code, down, pool):
    total = len(blocks) * blocks[0].shape[0]
    return resident_call(
        functools.partial(score_kernel, pool, len(blocks)), [((total // 2, LANES), jnp.float32)]
    )(*blocks, code, down)[0]


def place_kernel(pool, count, *refs):
    partial_refs, (code_ref, placed_ref) = refs[:count], refs[count:]
    ranks = partial_refs[0][...]
    for ref in partial_refs[1:]:
        ranks = ranks + ref[...]
    lines = ranks.shape[0]
    upper = lax.broadcasted_iota(jnp.int32, (lines, LANES), 1) >= ADAPTER_RANK
    turned = pltpu.roll(ranks, ADAPTER_RANK, 1)
    ranks = jnp.concatenate(
        [jnp.where(upper, turned, ranks), jnp.where(upper, ranks, turned)], axis=0
    )
    member = code_ref[...]
    upper = lax.broadcasted_iota(jnp.int32, ranks.shape, 1) >= ADAPTER_RANK
    placed = [
        jnp.where(member == jnp.where(upper, 2.0 * pair + 1.0, 2.0 * pair), ranks, 0.0)
        for pair in range(pool // 2)
    ]
    placed_ref[...] = jnp.concatenate(placed, axis=1).astype(jnp.bfloat16)


def raise_kernel(placed_ref, up_ref, *out_refs):
    raised = jnp.dot(placed_ref[...], up_ref[...], preferred_element_type=jnp.float32)
    raised = raised.astype(jnp.bfloat16)
    cap = out_refs[0].shape[0]
    for k, ref in enumerate(out_refs):
        ref[...] = raised[k * cap : (k + 1) * cap]


def raise_ranks(partials, code, up, cap, pool):
    outs = code.shape[0] // cap
    placed = resident_call(
        functools.partial(place_kernel, pool, len(partials)),
        [((code.shape[0], up.shape[0]), jnp.bfloat16)],
    )(*partials, code)[0]
    return resident_call(raise_kernel, [((cap, up.shape[1]), jnp.bfloat16)] * outs)(placed, up)


def join_kernel(spread_ref, base_ref, *refs):
    block_refs, out_ref = refs[:-1], refs[-1]
    blocks = jnp.concatenate([ref[...] for ref in block_refs], axis=0)
    update = jnp.dot(spread_ref[...], blocks, preferred_element_type=jnp.float32)
    out_ref[...] = (base_ref[...] + update).astype(out_ref.dtype)


def join(spread, base, blocks, dtype):
    if dtype == jnp.float32:
        return resident_call(join_kernel, [(base.shape, dtype)])(spread, base, *blocks)[0]
    return pl.pallas_call(
        join_kernel,
        in_specs=[IN_VMEM] * (2 + len(blocks)),
        out_shape=jax.ShapeDtypeStruct(base.shape, dtype),
        compiler_params=LIMIT,
    )(*map(resident, (spread, base, *blocks)))


def base_kernel(hidden_ref, weight_ref, out_ref):
    @pl.when(pl.program_id(0) == 0)
    def _():
        out_ref[...] = jnp.zeros_like(out_ref)

    out_ref[...] += jnp.dot(hidden_ref[...], weight_ref[...], preferred_element_type=jnp.float32)


def base_product(hidden, weight, steps):
    (rows, depth), columns = hidden.shape, weight.shape[1]
    step = depth // steps
    return pl.pallas_call(
        base_kernel,
        grid=(steps,),
        in_specs=[
            pl.BlockSpec((rows, step), lambda i: (0, i)),
            pl.BlockSpec((step, columns), lambda i: (i, 0)),
        ],
        out_specs=pl.BlockSpec((rows, columns), lambda i: (0, 0)),
        out_shape=jax.ShapeDtypeStruct((rows, columns), jnp.float32),
        compiler_params=LIMIT,
        name="base_product",
    )(stored(hidden), stored(weight))


def swap(value, axis, size, apart):
    return lax.ppermute(value, axis, [(i, i ^ apart) for i in range(size)])


def shards(
    n_ad, n_tp, hidden, key_value_weight, request_group, request_member, down, up
):
    rows = hidden.shape[0]
    width, pool = down.shape[0], down.shape[1] // ADAPTER_RANK
    cap = 2 * rows // n_ad
    half = n_ad // 2
    far = n_ad - 2 if n_ad > 2 else half
    far_down = swap(down, "ad", n_ad, far)
    near_spread, far_spread, *packed = pack(
        request_group.reshape(1, rows), request_member.reshape(1, rows), hidden, width, n_ad, far, cap
    )
    blocks, codes = packed[:n_ad], packed[n_ad:]
    near_rows = [blocks[0]] + [swap(blocks[k], "ad", n_ad, k) for k in range(1, half)]
    far_rows = [blocks[half]] + [swap(blocks[half + k], "ad", n_ad, k) for k in range(1, half)]
    codes = [codes[0]] + [swap(codes[k], "ad", n_ad, k) for k in range(1, half)]
    near_code, far_code = spread_codes(codes)
    base = base_product(hidden, key_value_weight, 4)
    base, *near_rows = lax.optimization_barrier((base, *near_rows))

    def spread_sum(partial):
        return [partial] + [swap(partial, "tp", n_tp, j) for j in range(1, n_tp)]

    def give_back(raised):
        back = [raised[0]]
        for k in range(1, half):
            back.append(swap(raised[k], "ad", n_ad, k))
        return back

    partial = score(near_rows, near_code, down, pool)
    partial, late_up = lax.optimization_barrier((partial, up))
    far_up = swap(late_up, "ad", n_ad, far)
    raised = raise_ranks(spread_sum(partial), near_code, up, cap, pool)
    base = join(near_spread, base, give_back(raised), jnp.float32)

    partial = score(far_rows, far_code, far_down, pool)
    raised = raise_ranks(spread_sum(partial), far_code, far_up, cap, pool)
    return join(far_spread, base, give_back(raised), jnp.bfloat16)


def solution(mesh):
    def step(*arrays):
        return shards(mesh.shape["ad"], mesh.shape["tp"], *arrays)

    placed = (P("ad", None), P(None, "tp"), P("ad", None), P("ad"), P("tp", "ad"), P("ad", "tp"))
    return jax.shard_map(step, mesh=mesh, in_specs=placed, out_specs=P("ad", "tp"), check_vma=False)
```

```python
import functools

import jax
import jax.numpy as jnp
from jax import lax
from jax.experimental import pallas as pl
from jax.experimental.pallas import tpu as pltpu
from jax.sharding import PartitionSpec as P


ADAPTER_RANK = 64
LANES = 128
LIMIT = pltpu.CompilerParams(vmem_limit_bytes=12 << 20)
IN_HBM = pl.BlockSpec(memory_space=pltpu.HBM)
IN_VMEM = pl.BlockSpec(memory_space=pltpu.VMEM)


def resident(value):
    return pltpu.with_memory_space_constraint(value, pltpu.VMEM)


def stored(value):
    return pltpu.with_memory_space_constraint(value, pltpu.HBM)


def resident_call(kernel, outs):
    def call(*operands):
        return pl.pallas_call(
            kernel,
            in_specs=[IN_VMEM] * len(operands),
            out_specs=[IN_VMEM] * len(outs),
            out_shape=[pltpu.VMEM(*out) for out in outs],
            compiler_params=LIMIT,
        )(*map(resident, operands))

    return call


def pack_kernel(
    n, far, cap, group_hbm, member_hbm, hidden_ref, near_ref, far_ref, *refs
):
    block_refs, code_refs = refs[:n], refs[n : n + n // 2]
    group_ref, member_ref, rows_ref, sems = refs[n + n // 2 :]
    rows, width = rows_ref.shape
    slots = n * cap
    half = n // 2
    at = pl.multiple_of(lax.axis_index("tp") * width, LANES)
    group_copy = pltpu.make_async_copy(group_hbm, group_ref, sems.at[0])
    member_copy = pltpu.make_async_copy(member_hbm, member_ref, sems.at[1])
    rows_copy = pltpu.make_async_copy(hidden_ref.at[:, pl.ds(at, width)], rows_ref, sems.at[2])
    group_copy.start()
    member_copy.start()
    rows_copy.start()
    group_copy.wait()
    group = group_ref[...]
    by_group = (lax.broadcasted_iota(jnp.int32, (LANES, rows), 0) == group).astype(jnp.float32)
    earlier = (
        lax.broadcasted_iota(jnp.int32, (rows, rows), 0)
        < lax.broadcasted_iota(jnp.int32, (rows, rows), 1)
    ).astype(jnp.bfloat16)
    before = jnp.dot(
        by_group.astype(jnp.bfloat16), earlier, preferred_element_type=jnp.float32
    )
    position = jnp.sum(by_group * before, axis=0, keepdims=True).astype(jnp.int32)
    apart = group ^ lax.axis_index("ad")
    slot = jnp.where(apart < half, apart, half + (apart ^ far)) * cap + position
    chosen = lax.broadcasted_iota(jnp.int32, (slots, rows), 0) == slot
    select = chosen.astype(jnp.bfloat16)
    member_copy.wait()
    member = jnp.broadcast_to(member_ref[...].astype(jnp.float32), (8, rows)).astype(jnp.bfloat16)
    code = lax.dot_general(
        member, select, (((1,), (1,)), ((), ())), preferred_element_type=jnp.float32
    )
    rows_copy.wait()
    packed = jnp.dot(select, rows_ref[...], preferred_element_type=jnp.float32)
    packed = packed.astype(jnp.bfloat16)
    for k, block_ref in enumerate(block_refs):
        block_ref[...] = packed[k * cap : (k + 1) * cap]
    for k, code_ref in enumerate(code_refs):
        code_ref[:, :cap] = code[:, k * cap : (k + 1) * cap]
        code_ref[:, cap:] = code[:, (half + k) * cap : (half + k + 1) * cap]
    column = jnp.transpose(jnp.broadcast_to(slot.astype(jnp.float32), (LANES, rows)))[:, :1]
    at_slot = lax.broadcasted_iota(jnp.int32, (rows, half * cap), 1).astype(jnp.float32)
    near_ref[...] = (at_slot == column).astype(jnp.bfloat16)
    far_ref[...] = (at_slot + float(half * cap) == column).astype(jnp.bfloat16)


def pack(group, member, hidden, width, n, far, cap):
    rows = hidden.shape[0]
    spread = pltpu.VMEM((rows, n // 2 * cap), jnp.bfloat16)
    block = pltpu.VMEM((cap, width), jnp.bfloat16)
    code = pltpu.VMEM((8, 2 * cap), jnp.float32)
    return pl.pallas_call(
        functools.partial(pack_kernel, n, far, cap),
        in_specs=[IN_HBM] * 3,
        out_specs=[IN_VMEM] * (2 + n + n // 2),
        out_shape=[spread] * 2 + [block] * n + [code] * (n // 2),
        scratch_shapes=[
            pltpu.VMEM((1, rows), jnp.int32),
            pltpu.VMEM((1, rows), jnp.int32),
            pltpu.VMEM((rows, width), jnp.bfloat16),
            pltpu.SemaphoreType.DMA((3,)),
        ],
        compiler_params=LIMIT,
        name="pack",
    )(*map(stored, (group, member, hidden)))


def code_kernel(*refs):
    code_refs, (near_ref, far_ref) = refs[:-2], refs[-2:]
    for k, ref in enumerate(code_refs):
        both = ref.shape[1]
        columns = jnp.transpose(jnp.broadcast_to(ref[:1, :], (LANES, both)))
        part = pl.ds(k * (both // 2), both // 2)
        near_ref[part, :] = columns[: both // 2]
        far_ref[part, :] = columns[both // 2 :]


def spread_codes(codes):
    total = len(codes) * codes[0].shape[1] // 2
    return resident_call(code_kernel, [((total, LANES), jnp.float32)] * 2)(*codes)


def score_kernel(pool, count, *refs):
    block_refs, (code_ref, down_ref, partial_ref) = refs[:count], refs[count:]
    rows = jnp.concatenate([ref[...] for ref in block_refs], axis=0)
    member = code_ref[...]
    scores = jnp.dot(rows, down_ref[...], preferred_element_type=jnp.float32)
    total = scores.shape[0]
    upper = lax.broadcasted_iota(jnp.int32, (total, LANES), 1) >= ADAPTER_RANK
    kept = jnp.zeros((total, LANES), jnp.float32)
    for pair in range(pool // 2):
        wanted = jnp.where(upper, 2.0 * pair + 1.0, 2.0 * pair)
        kept = kept + jnp.where(
            member == wanted, scores[:, pair * LANES : (pair + 1) * LANES], 0.0
        )
    both = kept + pltpu.roll(kept, ADAPTER_RANK, 1)
    partial_ref[...] = jnp.where(
        upper[: total // 2], both[total // 2 :], both[: total // 2]
    )


def score(blocks, code, down, pool):
    total = len(blocks) * blocks[0].shape[0]
    return resident_call(
        functools.partial(score_kernel, pool, len(blocks)), [((total // 2, LANES), jnp.float32)]
    )(*blocks, code, down)[0]


def place_kernel(pool, count, *refs):
    partial_refs, (code_ref, placed_ref) = refs[:count], refs[count:]
    ranks = partial_refs[0][...]
    for ref in partial_refs[1:]:
        ranks = ranks + ref[...]
    lines = ranks.shape[0]
    upper = lax.broadcasted_iota(jnp.int32, (lines, LANES), 1) >= ADAPTER_RANK
    turned = pltpu.roll(ranks, ADAPTER_RANK, 1)
    ranks = jnp.concatenate(
        [jnp.where(upper, turned, ranks), jnp.where(upper, ranks, turned)], axis=0
    )
    member = code_ref[...]
    upper = lax.broadcasted_iota(jnp.int32, ranks.shape, 1) >= ADAPTER_RANK
    placed = [
        jnp.where(member == jnp.where(upper, 2.0 * pair + 1.0, 2.0 * pair), ranks, 0.0)
        for pair in range(pool // 2)
    ]
    placed_ref[...] = jnp.concatenate(placed, axis=1).astype(jnp.bfloat16)


def raise_kernel(first, placed_ref, up_ref, *out_refs):
    cap = out_refs[0].shape[0]
    part = placed_ref[first * cap : (first + len(out_refs)) * cap]
    raised = jnp.dot(part, up_ref[...], preferred_element_type=jnp.float32)
    raised = raised.astype(jnp.bfloat16)
    for k, ref in enumerate(out_refs):
        ref[...] = raised[k * cap : (k + 1) * cap]


def raise_ranks(partials, code, up, cap, pool):
    outs = code.shape[0] // cap
    placed = resident_call(
        functools.partial(place_kernel, pool, len(partials)),
        [((code.shape[0], up.shape[0]), jnp.bfloat16)],
    )(*partials, code)[0]
    block = [((cap, up.shape[1]), jnp.bfloat16)]
    last = resident_call(functools.partial(raise_kernel, outs - 1), block)(placed, up)
    rest = resident_call(functools.partial(raise_kernel, 0), block * (outs - 1))(placed, up)
    return list(rest) + list(last)


def join_kernel(spread_ref, base_ref, *refs):
    block_refs, out_ref = refs[:-1], refs[-1]
    blocks = jnp.concatenate([ref[...] for ref in block_refs], axis=0)
    update = jnp.dot(spread_ref[...], blocks, preferred_element_type=jnp.float32)
    out_ref[...] = (base_ref[...] + update).astype(out_ref.dtype)


def join(spread, base, blocks, dtype):
    if dtype == jnp.float32:
        return resident_call(join_kernel, [(base.shape, dtype)])(spread, base, *blocks)[0]
    return pl.pallas_call(
        join_kernel,
        in_specs=[IN_VMEM] * (2 + len(blocks)),
        out_shape=jax.ShapeDtypeStruct(base.shape, dtype),
        compiler_params=LIMIT,
    )(*map(resident, (spread, base, *blocks)))


def base_kernel(hidden_ref, weight_ref, out_ref):
    @pl.when(pl.program_id(0) == 0)
    def _():
        out_ref[...] = jnp.zeros_like(out_ref)

    out_ref[...] += jnp.dot(hidden_ref[...], weight_ref[...], preferred_element_type=jnp.float32)


def base_product(hidden, weight, steps):
    (rows, depth), columns = hidden.shape, weight.shape[1]
    step = depth // steps
    return pl.pallas_call(
        base_kernel,
        grid=(steps,),
        in_specs=[
            pl.BlockSpec((rows, step), lambda i: (0, i)),
            pl.BlockSpec((step, columns), lambda i: (i, 0)),
        ],
        out_specs=pl.BlockSpec((rows, columns), lambda i: (0, 0)),
        out_shape=jax.ShapeDtypeStruct((rows, columns), jnp.float32),
        compiler_params=LIMIT,
        name="base_product",
    )(stored(hidden), stored(weight))


def swap(value, axis, size, apart):
    return lax.ppermute(value, axis, [(i, i ^ apart) for i in range(size)])


def shards(
    n_ad, n_tp, hidden, key_value_weight, request_group, request_member, down, up
):
    rows = hidden.shape[0]
    width, pool = down.shape[0], down.shape[1] // ADAPTER_RANK
    cap = 2 * rows // n_ad
    half = n_ad // 2
    far = n_ad - 2 if n_ad > 2 else half
    far_down = swap(down, "ad", n_ad, far)
    near_spread, far_spread, *packed = pack(
        request_group.reshape(1, rows), request_member.reshape(1, rows), hidden, width, n_ad, far, cap
    )
    blocks, codes = packed[:n_ad], packed[n_ad:]
    near_rows = [blocks[0]] + [swap(blocks[k], "ad", n_ad, k) for k in range(1, half)]
    far_rows = [blocks[half]] + [swap(blocks[half + k], "ad", n_ad, k) for k in range(1, half)]
    codes = [codes[0]] + [swap(codes[k], "ad", n_ad, k) for k in range(1, half)]
    near_code, far_code = spread_codes(codes)
    base = base_product(hidden, key_value_weight, 4)
    base, *near_rows = lax.optimization_barrier((base, *near_rows))

    def spread_sum(partial):
        return [partial] + [swap(partial, "tp", n_tp, j) for j in range(1, n_tp)]

    def give_back(raised):
        back = [raised[0]]
        for k in range(1, half):
            back.append(swap(raised[k], "ad", n_ad, k))
        return back

    partial = score(near_rows, near_code, down, pool)
    partial, late_up = lax.optimization_barrier((partial, up))
    far_up = swap(late_up, "ad", n_ad, far)
    raised = raise_ranks(spread_sum(partial), near_code, up, cap, pool)
    base = join(near_spread, base, give_back(raised), jnp.float32)

    partial = score(far_rows, far_code, far_down, pool)
    raised = raise_ranks(spread_sum(partial), far_code, far_up, cap, pool)
    return join(far_spread, base, give_back(raised), jnp.bfloat16)


def solution(mesh):
    def step(*arrays):
        return shards(mesh.shape["ad"], mesh.shape["tp"], *arrays)

    placed = (P("ad", None), P(None, "tp"), P("ad", None), P("ad"), P("tp", "ad"), P("ad", "tp"))
    return jax.shard_map(step, mesh=mesh, in_specs=placed, out_specs=P("ad", "tp"), check_vma=False)
```
